32 devices in a mesh: seq: 8 (over y, x, core), head: 4 (over z).
Axes of the slice: x: 2, y: 2, z: 4, core: 2. Of those that a mesh axis runs over, the one named last changes fastest.
Arguments:
- queries: bfloat16 [4096, 1536], P(('seq', 'head')), may hold values from -6.5 to 6.5
- key_states: bfloat16 [4096, 1536], P(('seq', 'head')), may hold values from -6.5 to 6.5
- value_states: bfloat16 [4096, 1536], P(('seq', 'head')), may hold values from -6 to 6
- grad_out: bfloat16 [4096, 1536], P(('seq', 'head')), may hold values from -6 to 6
- block_input: bfloat16 [4096, 1536], P(('seq', 'head')), may hold values from -45 to 45
- norm_gain: float32 [1536], replicated, may hold values from 0.1 to 1.9
- expert_ids: int32 [4096, 2], P(('seq', 'head')), may hold values from 0 to 7, all different within a row; in each aligned block of 128 rows (0 to 127, 128 to 255, ...) at most 36 rows name the same one
- gate_weights: bfloat16 [4096, 2], P(('seq', 'head')), may hold values from 0.19921875 to 1
- pre_act: bfloat16 [4096, 2, 3072], P(('seq', 'head')), may hold values from -6 to 6
- w_in: bfloat16 [8, 1536, 3072], P('seq', None, 'head'), may hold values from -0.15625 to 0.15625
- w_out: bfloat16 [8, 3072, 1536], P('seq', 'head'), may hold values from -0.109375 to 0.109375
Outputs:
- grad_q: bfloat16 [4096, 1536], P(('seq', 'head'))
- grad_k: bfloat16 [4096, 1536], P(('seq', 'head'))
- grad_v: bfloat16 [4096, 1536], P(('seq', 'head'))
- grad_input: bfloat16 [4096, 1536], P(('seq', 'head'))
- grad_w_in: bfloat16 [8, 1536, 3072], P('seq', None, 'head')
- grad_w_out: bfloat16 [8, 3072, 1536], P('seq', 'head')
The draws below stay inside these ranges and needn't reach their ends.
Inputs may be any that keep to these rules, and one draw needn't show every extreme that they name: `expert_ids`: each row names 2 different experts. Among the 128 tokens of one device (aligned blocks of rows) no expert is named by more than 36 tokens, and in every draw some expert is named by exactly 36 tokens of some device.
All inputs are finite; a program needn't handle non-finite values.
Results may differ from the reference program's by a relative error of at most 0.012.
The reference program's roundings to bfloat16 on the way count: a program that leaves them out, or rounds other values in their place, can miss the bound.
Values may be sent and summed in bfloat16 or wider, within the bound.
A program may use at most 128 MiB of HBM per device.

```python
import math
import jax
import jax.numpy as jnp
import numpy as np
from jax import lax

D = 1536
HEADS = 24
HD = 64
FF = 3072
TOP = 2
TOK_DEV = 128
LENGTH = 512
TOKENS = 4096
EXPERTS = 8
CAP = 36
N_SEQ = 8
N_HEAD = 4


def draw_queries(key, part):
    own_key = jax.random.fold_in(key, 21)
    values = jnp.clip(jax.random.normal(own_key, (TOKENS, D), jnp.float32), -5.0, 5.0)
    return values.astype(jnp.bfloat16)


def draw_key_states(key, part):
    own_key = jax.random.fold_in(key, 22)
    values = jnp.clip(jax.random.normal(own_key, (TOKENS, D), jnp.float32), -5.0, 5.0)
    return values.astype(jnp.bfloat16)


def draw_block_input(key, part):
    row_key = jax.random.fold_in(key, 31)
    col_key = jax.random.fold_in(key, 32)
    base_key = jax.random.fold_in(key, 33)
    row_scale = jnp.exp(jax.random.uniform(row_key, (TOKENS, 1), jnp.float32, math.log(0.3), math.log(3.0)))
    col_scale = jnp.exp(jax.random.uniform(col_key, (1, D), jnp.float32, math.log(0.3), math.log(3.0)))
    base = jnp.clip(jax.random.normal(base_key, (TOKENS, D), jnp.float32), -5.0, 5.0)
    values = row_scale * col_scale * base
    return values.astype(jnp.bfloat16)


def level_of(rng, dims, cuts, smallest, largest):
    loudness = 1.0
    for dim, shards_of in cuts:
        heights = jax.random.uniform(jax.random.fold_in(jax.random.fold_in(rng, 6), dim), (shards_of,), jnp.float32, smallest / len(cuts), largest / len(cuts))
        loudness = loudness * jnp.repeat(jnp.exp(heights), dims[dim] // shards_of).reshape((-1,) + (1,) * (len(dims) - 1 - dim))
    return loudness


def shared_out(key, own, number, rows, amount, top, most, lean):
    sequence = jax.random.permutation(key, amount)
    packed, usual = load_shares(amount, rows * top, most, lean, True), load_shares(amount, rows * top, most, lean, False)
    places = jnp.arange(amount)

    def named(tallies, turn):
        used = int((tallies > 0).sum())
        fixed = max(1, used // 4)
        moved = fixed + (places - fixed + turn * (used - fixed)) % max(1, amount - fixed)
        return jnp.zeros((amount,), jnp.int32).at[sequence[jnp.where(places < fixed, places, moved)]].set(jnp.asarray(tallies, jnp.int32))

    tallies = jnp.where(number % 4 == 0, named(packed, number // 4), named(usual, number - number // 4 - 1))
    mixed = jax.random.permutation(jax.random.fold_in(own, 3), amount)
    donor, sink = mixed[0:amount // 2 * 2:2], mixed[1:amount // 2 * 2:2]
    margin = jnp.minimum(tallies[donor] - 1, most - tallies[sink]) // 2
    margin = jnp.where((donor == sequence[0]) | (sink == sequence[0]) | (tallies[sink] == 0), 0, jnp.maximum(margin, 0))
    moved = jax.random.randint(jax.random.fold_in(own, 4), (amount // 2,), 0, 1 << 20) % (margin + 1)
    tallies = tallies.at[donor].add(-moved).at[sink].add(moved)
    items = jnp.searchsorted(jnp.cumsum(tallies), jnp.arange(rows * top), side="right").astype(jnp.int32)
    listing = items.reshape(top, rows).T
    listing = listing[jax.random.permutation(jax.random.fold_in(own, 1), rows)]
    turn = jax.random.randint(jax.random.fold_in(own, 2), (rows, 1), 0, top)
    return jnp.take_along_axis(listing, (jnp.arange(top)[None, :] + turn) % top, axis=1)


def load_shares(number_of, total, most, skew, full):
    loads = [(1 << 20) // math.isqrt(standing ** skew) + 1 for standing in range(1, number_of + 1)]
    largest = most if full else min(most, max(-(-total // number_of), total * loads[0] // sum(loads)))
    least = 1 if total - largest >= number_of - 1 else 0
    counts, rest = [largest] + [least] * (number_of - 1), total - largest - least * (number_of - 1)
    while rest > 0:
        free = [i for i in range(1, number_of) if counts[i] < largest] or [i for i in range(1, number_of) if counts[i] < most]
        whole, left = sum([loads[i] for i in free]), rest
        for i in free:
            more = min(most - counts[i], max(1, left * loads[i] // whole), rest)
            counts[i] = counts[i] + more
            rest = rest - more
    return np.array(counts)


def bell_draw(key, shape, spread, most, pieces=(), held_as=jnp.bfloat16):
    drawn = jax.random.normal(key, shape, jnp.float32) * spread
    if len(pieces) > 0:
        drawn = level_of(key, shape, pieces, -0.22, 0.18) * drawn
    return jnp.clip(drawn, min=-most, max=most).astype(held_as)


def setup_inputs(seed: int = 0) -> dict:
    keys = jax.random.split(jax.random.key(seed), 12)
    queries = draw_queries(jax.random.fold_in(keys[11], 71), 0)
    key_states = draw_key_states(jax.random.fold_in(keys[11], 71), 0)
    value_states = bell_draw(keys[2], (TOKENS, D), 1.0, 6.0, ((0, 32),))
    grad_out = bell_draw(keys[3], (TOKENS, D), 1.0, 6.0, ((0, 32),))
    block_input = draw_block_input(jax.random.fold_in(keys[11], 71), 0)
    norm_gain = jnp.clip(1.0 + 0.18 * jax.random.normal(keys[5], (D,), jnp.float32), 0.1, 1.9)
    expert_ids_keys = jax.random.split(jax.random.fold_in(keys[6], 1), TOKENS // TOK_DEV)
    expert_ids_turns = jax.random.permutation(jax.random.fold_in(keys[6], 3), TOKENS // TOK_DEV)
    expert_ids = jax.vmap(lambda own, number: shared_out(jax.random.fold_in(keys[6], 2), own, number, TOK_DEV, EXPERTS, TOP, CAP, 2))(expert_ids_keys, expert_ids_turns).reshape((TOKENS, TOP))
    gate_weights = jnp.clip(0.19921875 + 0.80078125 * jax.random.uniform(keys[7], (TOKENS, TOP), jnp.float32) ** level_of(keys[7], (TOKENS, TOP), ((0, 32),), -0.2, 0.2), 0.19921875, 1.0).astype(jnp.bfloat16)
    pre_act = bell_draw(keys[8], (TOKENS, TOP, FF), 1.0, 6.0, ((0, 32),))
    w_in = bell_draw(keys[9], (EXPERTS, D, FF), D ** -0.5, 0.15625, ((0, 8), (2, 4)))
    w_out = bell_draw(keys[10], (EXPERTS, FF, D), FF ** -0.5, 0.109375, ((0, 8), (1, 4)))
    return {"queries": queries, "key_states": key_states, "value_states": value_states, "grad_out": grad_out, "block_input": block_input, "norm_gain": norm_gain, "expert_ids": expert_ids, "gate_weights": gate_weights, "pre_act": pre_act, "w_in": w_in, "w_out": w_out}


tanh_coeff = 0.7978845608028654
cubic_coeff = 0.044715

def gelu_pair(values):
    inner = tanh_coeff * (values + cubic_coeff * values * values * values)
    tangent = jnp.tanh(inner)
    output = 0.5 * values * (1.0 + tangent)
    slope = 0.5 * (1.0 + tangent) + 0.5 * values * (1.0 - tangent * tangent) * tanh_coeff * (1.0 + 3.0 * cubic_coeff * values * values)
    return (output, slope)

def rounded(values):
    return lax.optimization_barrier(values.astype(jnp.bfloat16)).astype(jnp.float32)

def attend_sequence(members):
    query_s, key_s, value_s, grad_s = [member.reshape(LENGTH, HEADS, HD).astype(jnp.float32) for member in members]
    score_scale = 1.0 / math.sqrt(HD)
    scores = jnp.einsum('qhd,khd->hqk', query_s, key_s) * score_scale
    row_peak = lax.optimization_barrier(jnp.max(scores, axis=2, keepdims=True))
    exp_scores = jnp.exp(scores - row_peak)
    soft_probs = exp_scores / lax.optimization_barrier(jnp.sum(exp_scores, axis=2, keepdims=True))
    probs_b = rounded(soft_probs)
    attended = jnp.einsum('hqk,khd->qhd', probs_b, value_s)
    row_delta = lax.optimization_barrier(jnp.sum(grad_s * attended, axis=2))
    grad_probs = jnp.einsum('qhd,khd->hqk', grad_s, value_s)
    grad_scores = rounded(soft_probs * (grad_probs - row_delta.T[:, :, None]))
    grad_query = (jnp.einsum('hqk,khd->qhd', grad_scores, key_s) * score_scale).astype(jnp.bfloat16)
    grad_key = (jnp.einsum('hqk,qhd->khd', grad_scores, query_s) * score_scale).astype(jnp.bfloat16)
    grad_value = jnp.einsum('hqk,qhd->khd', probs_b, grad_s).astype(jnp.bfloat16)
    return tuple((member.reshape(LENGTH, D) for member in (grad_query, grad_key, grad_value)))

def reference(queries, key_states, value_states, grad_out, block_input, norm_gain, expert_ids, gate_weights, pre_act, w_in, w_out):
    seq_count = TOKENS // LENGTH
    stacked = tuple((member.reshape(seq_count, LENGTH, D) for member in (queries, key_states, value_states, grad_out)))
    grad_q, grad_k, grad_v = lax.map(attend_sequence, stacked)
    grad_q = grad_q.reshape(TOKENS, D)
    grad_k = grad_k.reshape(TOKENS, D)
    grad_v = grad_v.reshape(TOKENS, D)
    input_f = block_input.astype(jnp.float32)
    inv_rms = 1.0 / jnp.sqrt(lax.optimization_barrier(jnp.mean(input_f * input_f, axis=1, keepdims=True)) + 1e-05)
    scaled_in = input_f * inv_rms
    normed = (scaled_in * norm_gain[None, :]).astype(jnp.bfloat16)
    flat_ids = expert_ids.reshape(-1)
    flat_gate = gate_weights.reshape(-1).astype(jnp.float32)
    flat_pre = pre_act.reshape(TOKENS * TOP, FF)
    rows_max = N_SEQ * N_HEAD * CAP
    group_width = FF // N_HEAD
    total_assign = TOKENS * TOP

    def per_expert(assigned, expert):
        chosen = jnp.nonzero(flat_ids == expert, size=rows_max, fill_value=total_assign)[0].astype(jnp.int32)
        valid = chosen < total_assign
        safe_idx = jnp.where(valid, chosen, jnp.zeros_like(chosen))
        token_of = safe_idx // TOP
        gate_col = jnp.where(valid, flat_gate[safe_idx], jnp.zeros_like(flat_gate[safe_idx]))[:, None]
        rows_x = normed[token_of]
        rows_grad = grad_out[token_of]
        rows_pre = flat_pre[safe_idx].astype(jnp.float32)
        activ, slope = gelu_pair(rows_pre)
        hidden_g = (gate_col * activ).astype(jnp.bfloat16)
        gw_out = jnp.dot(hidden_g.T, rows_grad, preferred_element_type=jnp.float32).astype(jnp.bfloat16)
        back_act = jnp.dot(rows_grad, w_out[expert].T, preferred_element_type=jnp.float32)
        grad_pre = (gate_col * back_act * slope).astype(jnp.bfloat16)
        gw_in = jnp.dot(rows_x.T, grad_pre, preferred_element_type=jnp.float32).astype(jnp.bfloat16)
        partials = jnp.einsum('rjf,djf->jrd', grad_pre.reshape(rows_max, N_HEAD, group_width).astype(jnp.float32), w_in[expert].reshape(D, N_HEAD, group_width).astype(jnp.float32))
        summed = lax.optimization_barrier(jnp.sum(rounded(partials), axis=0)).astype(jnp.bfloat16)
        assigned = assigned.at[chosen].set(summed, mode='drop')
        return (assigned, (gw_in, gw_out))
    assigned, (grad_w_in, grad_w_out) = lax.scan(per_expert, jnp.zeros((total_assign, D), jnp.bfloat16), jnp.arange(EXPERTS, dtype=jnp.int32))
    grad_normed = lax.optimization_barrier(jnp.sum(assigned.reshape(TOKENS, TOP, D).astype(jnp.float32), axis=1))
    scaled_grad = norm_gain[None, :] * grad_normed
    grad_input = (inv_rms * (scaled_grad - scaled_in * lax.optimization_barrier(jnp.mean(scaled_grad * scaled_in, axis=1, keepdims=True)))).astype(jnp.bfloat16)
    return (grad_q, grad_k, grad_v, grad_input, grad_w_in, grad_w_out)
```

```python
import math

import jax
import jax.numpy as jnp
from jax import lax
from jax.sharding import PartitionSpec as P

HD = 64


tanh_coeff = 0.7978845608028654
cubic_coeff = 0.044715
ROWS = (((0,), (0,)), ((), ()))
COLS = (((1,), (1,)), ((), ()))


def gelu_pair(values):
    inner = tanh_coeff * (values + cubic_coeff * values * values * values)
    tangent = jnp.tanh(inner)
    output = 0.5 * values * (1.0 + tangent)
    slope = 0.5 * (1.0 + tangent) + 0.5 * values * (1.0 - tangent * tangent) * tanh_coeff * (
        1.0 + 3.0 * cubic_coeff * values * values
    )
    return (output, slope)


def from_head(block, shift):
    size = lax.axis_size("head")
    return lax.ppermute(block, "head", [(i, (i - shift) % size) for i in range(size)])


def to_head(block, shift):
    return from_head(block, -shift)


def gather_head(block):
    size = lax.axis_size("head")
    if size != 4:
        return [block] + [from_head(block, j) for j in range(1, size)]
    half = block.shape[0] // 2
    after, before = from_head(block, 1), from_head(block, 3)
    far = jnp.concatenate([from_head(after[:half], 1), from_head(before[half:], 3)], axis=0)
    return [block, after, far, before]


def columns_of(block, group):
    size = lax.axis_size("head")
    width = block.shape[1] // size
    return lax.dynamic_index_in_dim(
        jnp.stack([block[:, i * width : (i + 1) * width] for i in range(size)]), group, 0, False
    )


def spread_head(block):
    size = lax.axis_size("head")
    me = lax.axis_index("head")
    return [columns_of(block, me)] + [
        from_head(columns_of(block, (me - j) % size), j) for j in range(1, size)
    ]


def unspread_head(blocks):
    size = lax.axis_size("head")
    me = lax.axis_index("head")
    came = jnp.stack([blocks[0]] + [to_head(blocks[j], j) for j in range(1, size)])
    return jnp.concatenate(
        [lax.dynamic_index_in_dim(came, (me - group) % size, 0, False) for group in range(size)],
        axis=1,
    )


def swap_seq(table):
    size = lax.axis_size("seq")
    rows = table.shape[0] // size
    return [table[:rows]] + [
        lax.ppermute(table[k * rows : (k + 1) * rows], "seq", [(i, i ^ k) for i in range(size)])
        for k in range(1, size)
    ]


def attend(query_all, key_all, value_all, grad_all, head_dim):
    length = query_all.shape[0]
    heads_here = query_all.shape[1] // head_dim
    query_h = query_all.reshape(length, heads_here, head_dim)
    key_h = key_all.reshape(length, heads_here, head_dim)
    value_h = value_all.reshape(length, heads_here, head_dim)
    grad_h = grad_all.reshape(length, heads_here, head_dim)
    score_scale = 1.0 / math.sqrt(head_dim)
    scores = (
        jnp.einsum("qhd,khd->hqk", query_h, key_h, preferred_element_type=jnp.float32)
        * score_scale
    )
    row_peak = jnp.max(scores, axis=2, keepdims=True)
    exp_scores = jnp.exp(scores - row_peak)
    soft_probs = exp_scores / jnp.sum(exp_scores, axis=2, keepdims=True)
    probs_b = soft_probs.astype(jnp.bfloat16)
    attended = jnp.einsum("hqk,khd->qhd", probs_b, value_h, preferred_element_type=jnp.float32)
    row_delta = jnp.sum(grad_h.astype(jnp.float32) * attended, axis=2)
    grad_probs = jnp.einsum("qhd,khd->hqk", grad_h, value_h, preferred_element_type=jnp.float32)
    grad_scores = (soft_probs * (grad_probs - row_delta.T[:, :, None])).astype(jnp.bfloat16)
    grad_query = jnp.einsum("hqk,khd->qhd", grad_scores, key_h, preferred_element_type=jnp.float32)
    grad_key = jnp.einsum("hqk,qhd->khd", grad_scores, query_h, preferred_element_type=jnp.float32)
    grad_value = jnp.einsum("hqk,qhd->khd", probs_b, grad_h, preferred_element_type=jnp.float32)
    return tuple(
        member.astype(jnp.bfloat16).reshape(length, heads_here * head_dim)
        for member in (grad_query * score_scale, grad_key * score_scale, grad_value)
    )


def slot_tables(flat_ids, gates, experts, capacity, per_token):
    relative = flat_ids ^ lax.axis_index("seq")
    onehot = (relative[:, None] == jnp.arange(experts)[None, :]).astype(jnp.float32)
    count = flat_ids.shape[0]
    earlier = (jnp.arange(count)[None, :] <= jnp.arange(count)[:, None]).astype(jnp.bfloat16)
    running = jnp.dot(earlier, onehot.astype(jnp.bfloat16), preferred_element_type=jnp.float32)
    position = jnp.sum(running * onehot, axis=1).astype(jnp.int32) - 1
    target = relative * capacity + position
    slots = jnp.arange(experts * capacity)[:, None]
    assign = (target[None, :] == slots).astype(jnp.bfloat16)
    by_choice = target.reshape(-1, per_token)
    gate_of = gates.reshape(-1, per_token)
    token, weighted = 0.0, 0.0
    for c in range(per_token):
        hit = by_choice[:, c][None, :] == slots
        token = token + jnp.where(hit, 1.0, 0.0)
        weighted = weighted + jnp.where(hit, gate_of[:, c][None, :], 0.0)
    return (assign, token.astype(jnp.bfloat16), weighted.astype(jnp.bfloat16))


def pick(table, rows):
    return jnp.dot(table, rows, preferred_element_type=jnp.float32).astype(jnp.bfloat16)


def shards(
    queries,
    key_states,
    value_states,
    grad_out,
    block_input,
    norm_gain,
    expert_ids,
    gate_weights,
    pre_act,
    w_in,
    w_out,
):
    experts = lax.axis_size("seq")
    heads = lax.axis_size("head")
    head = lax.axis_index("head")
    tokens_here, width = queries.shape
    per_token = expert_ids.shape[1]
    capacity = heads * (9 * tokens_here * per_token // (8 * experts))
    capacity = -(-capacity // 16) * 16

    routing = jnp.concatenate(
        [expert_ids.astype(jnp.float32), gate_weights.astype(jnp.float32)], axis=1
    ).T
    routing = jnp.concatenate([routing] + [from_head(routing, j) for j in range(1, heads)], axis=1)
    ids_all = routing[:per_token].T.astype(jnp.int32).reshape(-1)
    gates_all = routing[per_token:].T.reshape(-1)

    grad_slots = gather_head(grad_out)
    grad_rows = jnp.concatenate(grad_slots, axis=0)
    hidden_all = pre_act.shape[2]
    pre_slots = jnp.concatenate(spread_head(pre_act.reshape(-1, hidden_all)), axis=0)
    input_f = block_input.astype(jnp.float32)
    inv_rms = lax.rsqrt(jnp.mean(input_f * input_f, axis=1, keepdims=True) + 1e-05)
    scaled_in = input_f * inv_rms
    normed = (scaled_in * norm_gain[None, :]).astype(jnp.bfloat16)
    normed_rows = jnp.concatenate(gather_head(normed), axis=0)

    assign_table, token_table, gate_table = slot_tables(
        ids_all, gates_all, experts, capacity, per_token
    )
    rows_grad = jnp.concatenate(swap_seq(pick(gate_table, grad_rows)), axis=0)
    pre_flat = jnp.concatenate(swap_seq(pick(assign_table, pre_slots)), axis=0)
    rows_x = jnp.concatenate(swap_seq(pick(token_table, normed_rows)), axis=0)

    query_all = jnp.concatenate(spread_head(queries), axis=0)
    key_all = jnp.concatenate(spread_head(key_states), axis=0)
    value_all = jnp.concatenate(spread_head(value_states), axis=0)
    grad_all = columns_of(grad_rows, head)
    back = attend(query_all, key_all, value_all, grad_all, HD)
    grad_q, grad_k, grad_v = (
        unspread_head([member[j * tokens_here : (j + 1) * tokens_here] for j in range(heads)])
        for member in back
    )

    activ, slope = gelu_pair(pre_flat.astype(jnp.float32))
    back_act = lax.dot_general(rows_grad, w_out[0], COLS, preferred_element_type=jnp.float32)
    grad_pre = (back_act * slope).astype(jnp.bfloat16)
    partial = lax.dot_general(
        grad_pre, w_in[0], COLS, preferred_element_type=jnp.float32
    ).astype(jnp.bfloat16)
    came_back = jnp.concatenate(swap_seq(partial), axis=0)
    grad_w_out = lax.dot_general(
        activ.astype(jnp.bfloat16), rows_grad, ROWS, preferred_element_type=jnp.float32
    ).astype(jnp.bfloat16)[None]
    grad_w_in = lax.dot_general(
        rows_x, grad_pre, ROWS, preferred_element_type=jnp.float32
    ).astype(jnp.bfloat16)[None]

    token_sums = lax.dot_general(
        token_table, came_back, ROWS, preferred_element_type=jnp.float32
    ).astype(jnp.bfloat16)
    pieces = [token_sums[j * tokens_here : (j + 1) * tokens_here] for j in range(heads)]
    grad_normed = pieces[0].astype(jnp.float32)
    for j in range(1, heads):
        grad_normed = grad_normed + to_head(pieces[j], j).astype(jnp.float32)
    scaled_grad = norm_gain[None, :] * grad_normed
    grad_input = (
        inv_rms
        * (scaled_grad - scaled_in * jnp.mean(scaled_grad * scaled_in, axis=1, keepdims=True))
    ).astype(jnp.bfloat16)
    return (grad_q, grad_k, grad_v, grad_input, grad_w_in, grad_w_out)


def solution(mesh):
    return jax.shard_map(
        shards,
        mesh=mesh,
        in_specs=(
            P(("seq", "head"), None),
            P(("seq", "head"), None),
            P(("seq", "head"), None),
            P(("seq", "head"), None),
            P(("seq", "head"), None),
            P(),
            P(("seq", "head"), None),
            P(("seq", "head"), None),
            P(("seq", "head"), None, None),
            P("seq", None, "head"),
            P("seq", "head", None),
        ),
        out_specs=(
            P(("seq", "head"), None),
            P(("seq", "head"), None),
            P(("seq", "head"), None),
            P(("seq", "head"), None),
            P("seq", None, "head"),
            P("seq", "head", None),
        ),
        check_vma=False,
    )
```

```python
import math

import jax
import jax.numpy as jnp
from jax import lax
from jax.experimental import pallas as pl
from jax.experimental.pallas import tpu as pltpu
from jax.sharding import PartitionSpec as P

HD = 64


tanh_coeff = 0.7978845608028654
cubic_coeff = 0.044715
ROWS = (((0,), (0,)), ((), ()))
COLS = (((1,), (1,)), ((), ()))


def gelu_pair(values):
    inner = tanh_coeff * (values + cubic_coeff * values * values * values)
    tangent = jnp.tanh(inner)
    output = 0.5 * values * (1.0 + tangent)
    slope = 0.5 * (1.0 + tangent) + 0.5 * values * (1.0 - tangent * tangent) * tanh_coeff * (
        1.0 + 3.0 * cubic_coeff * values * values
    )
    return (output, slope)


def from_head(block, shift):
    size = lax.axis_size("head")
    return lax.ppermute(block, "head", [(i, (i - shift) % size) for i in range(size)])


def to_head(block, shift):
    return from_head(block, -shift)


def gather_head(block):
    size = lax.axis_size("head")
    if size != 4:
        return [block] + [from_head(block, j) for j in range(1, size)]
    half = block.shape[0] // 2
    after, before = from_head(block, 1), from_head(block, 3)
    far = jnp.concatenate([from_head(after[:half], 1), from_head(before[half:], 3)], axis=0)
    return [block, after, far, before]


def local_call(body, outs, *args, scratch=()):
    space = pl.BlockSpec(memory_space=pltpu.VMEM)
    return pl.pallas_call(
        body,
        out_shape=tuple(jax.ShapeDtypeStruct(shape, jnp.bfloat16) for shape in outs),
        in_specs=[space] * len(args),
        out_specs=tuple([space] * len(outs)),
        scratch_shapes=list(scratch),
        compiler_params=pltpu.CompilerParams(vmem_limit_bytes=48 * 1024 * 1024),
    )(*args)


def join(blocks):
    rows, width = blocks[0].shape
    count = len(blocks)

    def body(*refs):
        for k in range(count):
            refs[count][k * rows : (k + 1) * rows] = refs[k][...]

    return local_call(body, [(rows * count, width)], *blocks)[0]


def at_group(group, size, part, copy):
    if part % 128 == 0:
        copy(pl.ds(pl.multiple_of(group * part, part), part))
        return
    for g in range(size):

        @pl.when(group == g)
        def _(g=g):
            copy(slice(g * part, (g + 1) * part))


def split_columns(arrays, size):
    rows, width = arrays[0].shape
    part = width // size
    count = len(arrays)

    def body(*refs):
        me = lax.axis_index("head")
        for j in range(size):
            group = lax.rem(me + (size - j), size)

            def copy(columns, j=j):
                for i in range(count):
                    refs[count + j][i * rows : (i + 1) * rows] = refs[i][:, columns]

            at_group(group, size, part, copy)

    return local_call(body, [(rows * count, part)] * size, *arrays)


def spread_head(arrays):
    size = lax.axis_size("head")
    blocks = split_columns(arrays, size)
    return [blocks[0]] + [from_head(blocks[j], j) for j in range(1, size)]


def join_members(slots, count):
    size = len(slots)
    rows, width = slots[0].shape[0] // count, slots[0].shape[1]

    def body(*refs):
        for i in range(count):
            for j in range(size):
                refs[size + i][j * rows : (j + 1) * rows] = refs[j][i * rows : (i + 1) * rows]

    return local_call(body, [(rows * size, width)] * count, *slots)


def return_head(members):
    size = lax.axis_size("head")
    count = len(members)
    rows, width = members[0].shape[0] // size, members[0].shape[1]

    def cut(*refs):
        for j in range(size):
            for i in range(count):
                refs[count + j][i * rows : (i + 1) * rows] = refs[i][j * rows : (j + 1) * rows]

    blocks = local_call(cut, [(rows * count, width)] * size, *members)
    came = [blocks[0]] + [to_head(blocks[j], j) for j in range(1, size)]

    def place(*refs):
        me = lax.axis_index("head")
        for j in range(size):
            group = lax.rem(me + (size - j), size)

            def copy(columns, j=j):
                for i in range(count):
                    refs[size + i][:, columns] = refs[j][i * rows : (i + 1) * rows]

            at_group(group, size, width, copy)

    return local_call(place, [(rows, width * size)] * count, *came)


def deal(table, rows, parts):
    size = table.shape[0] // parts

    def body(table_ref, rows_ref, *outs):
        for k in range(parts):
            outs[k][...] = jnp.dot(
                table_ref[k * size : (k + 1) * size],
                rows_ref[...],
                preferred_element_type=jnp.float32,
            ).astype(jnp.bfloat16)

    return local_call(body, [(size, rows.shape[1])] * parts, table, rows)


def swap_seq(blocks):
    size = len(blocks)
    return [blocks[0]] + [
        lax.ppermute(blocks[k], "seq", [(i, i ^ k) for i in range(size)]) for k in range(1, size)
    ]


def expert_middle(grads, pres, w_out, w_in):
    count = len(grads)
    rows, width = grads[0].shape
    hidden = pres[0].shape[1]

    def body(*refs):
        ins, rest = refs[: 2 * count], refs[2 * count :]
        out_ref, in_ref, rest = rest[0], rest[1], rest[2:]
        downs, rest = rest[:count], rest[count:]
        grad_all, act_all, gpre_all = rest
        for k in range(count):
            here = slice(k * rows, (k + 1) * rows)
            grad = ins[k][...]
            grad_all[here] = grad
            activ, slope = gelu_pair(ins[count + k][...].astype(jnp.float32))
            act_all[here] = activ.astype(jnp.bfloat16)
            back = lax.dot_general(grad, out_ref[...], COLS, preferred_element_type=jnp.float32)
            gpre = (back * slope).astype(jnp.bfloat16)
            gpre_all[here] = gpre
            downs[k][...] = lax.dot_general(
                gpre, in_ref[...], COLS, preferred_element_type=jnp.float32
            ).astype(jnp.bfloat16)

    total = rows * count
    outs = [(rows, width)] * count + [(total, width), (total, hidden), (total, hidden)]
    got = local_call(body, outs, *grads, *pres, w_out, w_in)
    return (got[:count], *got[count:])


def attend(query_all, key_all, value_all, grad_all, head_dim):
    length = query_all.shape[0]
    heads_here = query_all.shape[1] // head_dim
    query_h = query_all.reshape(length, heads_here, head_dim)
    key_h = key_all.reshape(length, heads_here, head_dim)
    value_h = value_all.reshape(length, heads_here, head_dim)
    grad_h = grad_all.reshape(length, heads_here, head_dim)
    score_scale = 1.0 / math.sqrt(head_dim)
    scores = (
        jnp.einsum("qhd,khd->hqk", query_h, key_h, preferred_element_type=jnp.float32)
        * score_scale
    )
    row_peak = jnp.max(scores, axis=2, keepdims=True)
    exp_scores = jnp.exp(scores - row_peak)
    soft_probs = exp_scores / jnp.sum(exp_scores, axis=2, keepdims=True)
    probs_b = soft_probs.astype(jnp.bfloat16)
    attended = jnp.einsum("hqk,khd->qhd", probs_b, value_h, preferred_element_type=jnp.float32)
    row_delta = jnp.sum(grad_h.astype(jnp.float32) * attended, axis=2)
    grad_probs = jnp.einsum("qhd,khd->hqk", grad_h, value_h, preferred_element_type=jnp.float32)
    grad_scores = (soft_probs * (grad_probs - row_delta.T[:, :, None])).astype(jnp.bfloat16)
    grad_query = jnp.einsum("hqk,khd->qhd", grad_scores, key_h, preferred_element_type=jnp.float32)
    grad_key = jnp.einsum("hqk,qhd->khd", grad_scores, query_h, preferred_element_type=jnp.float32)
    grad_value = jnp.einsum("hqk,qhd->khd", probs_b, grad_h, preferred_element_type=jnp.float32)
    return tuple(
        member.astype(jnp.bfloat16).reshape(length, heads_here * head_dim)
        for member in (grad_query * score_scale, grad_key * score_scale, grad_value)
    )


def slot_tables(flat_ids, gates, experts, capacity, per_token):
    relative = flat_ids ^ lax.axis_index("seq")
    onehot = (relative[:, None] == jnp.arange(experts)[None, :]).astype(jnp.float32)
    count = flat_ids.shape[0]
    earlier = (jnp.arange(count)[None, :] <= jnp.arange(count)[:, None]).astype(jnp.bfloat16)
    running = jnp.dot(earlier, onehot.astype(jnp.bfloat16), preferred_element_type=jnp.float32)
    position = jnp.sum(running * onehot, axis=1).astype(jnp.int32) - 1
    target = relative * capacity + position
    slots = jnp.arange(experts * capacity)[:, None]
    assign = (target[None, :] == slots).astype(jnp.bfloat16)
    by_choice = target.reshape(-1, per_token)
    gate_of = gates.reshape(-1, per_token)
    token, weighted = 0.0, 0.0
    for c in range(per_token):
        hit = by_choice[:, c][None, :] == slots
        token = token + jnp.where(hit, 1.0, 0.0)
        weighted = weighted + jnp.where(hit, gate_of[:, c][None, :], 0.0)
    return (assign, token.astype(jnp.bfloat16), weighted.astype(jnp.bfloat16))


def shards(
    queries,
    key_states,
    value_states,
    grad_out,
    block_input,
    norm_gain,
    expert_ids,
    gate_weights,
    pre_act,
    w_in,
    w_out,
):
    experts = lax.axis_size("seq")
    heads = lax.axis_size("head")
    head = lax.axis_index("head")
    tokens_here, width = queries.shape
    per_token = expert_ids.shape[1]
    capacity = heads * (9 * tokens_here * per_token // (8 * experts))
    capacity = -(-capacity // 16) * 16

    routing = jnp.concatenate(
        [expert_ids.astype(jnp.float32), gate_weights.astype(jnp.float32)], axis=1
    ).T
    routing = jnp.concatenate([routing] + [from_head(routing, j) for j in range(1, heads)], axis=1)
    ids_all = routing[:per_token].T.astype(jnp.int32).reshape(-1)
    gates_all = routing[per_token:].T.reshape(-1)

    grad_slots = gather_head(grad_out)
    grad_rows = jnp.concatenate(grad_slots, axis=0)
    hidden_all = pre_act.shape[2]
    pre_own = pre_act.reshape(-1, hidden_all)
    input_f = block_input.astype(jnp.float32)
    inv_rms = lax.rsqrt(jnp.mean(input_f * input_f, axis=1, keepdims=True) + 1e-05)
    scaled_in = input_f * inv_rms
    normed = (scaled_in * norm_gain[None, :]).astype(jnp.bfloat16)

    assign_table, token_table, gate_table = slot_tables(
        ids_all, gates_all, experts, capacity, per_token
    )
    grad_blocks = deal(gate_table, grad_rows, experts)
    pre_own, _ = lax.optimization_barrier((pre_own, grad_slots[2]))
    grads = swap_seq(grad_blocks)
    pre_slots = join(spread_head([pre_own]))
    normed, pre_slots = lax.optimization_barrier((normed, pre_slots))
    pres = swap_seq(deal(assign_table, pre_slots, experts))

    query_all, key_all, value_all = join_members(
        spread_head([queries, key_states, value_states]), 3
    )
    part = width // heads
    grad_all = lax.dynamic_slice_in_dim(grad_rows, head * part, part, 1)
    back = attend(query_all, key_all, value_all, grad_all, HD)
    normed_rows = jnp.concatenate(gather_head(normed), axis=0)

    downs, rows_grad, activ, grad_pre = expert_middle(grads, pres, w_out[0], w_in[0])
    x_blocks = deal(token_table, normed_rows, experts)
    x_blocks, downs = lax.optimization_barrier((x_blocks, downs))
    came_back = join(swap_seq(downs))
    rows_x = join(swap_seq(x_blocks))
    grad_q, grad_k, grad_v = return_head(back)
    grad_w_out = lax.dot_general(
        activ, rows_grad, ROWS, preferred_element_type=jnp.float32
    ).astype(jnp.bfloat16)[None]
    grad_w_in = lax.dot_general(
        rows_x, grad_pre, ROWS, preferred_element_type=jnp.float32
    ).astype(jnp.bfloat16)[None]

    token_sums = lax.dot_general(
        token_table, came_back, ROWS, preferred_element_type=jnp.float32
    ).astype(jnp.bfloat16)
    pieces = [token_sums[j * tokens_here : (j + 1) * tokens_here] for j in range(heads)]
    grad_normed = pieces[0].astype(jnp.float32)
    for j in range(1, heads):
        grad_normed = grad_normed + to_head(pieces[j], j).astype(jnp.float32)
    scaled_grad = norm_gain[None, :] * grad_normed
    grad_input = (
        inv_rms
        * (scaled_grad - scaled_in * jnp.mean(scaled_grad * scaled_in, axis=1, keepdims=True))
    ).astype(jnp.bfloat16)
    return (grad_q, grad_k, grad_v, grad_input, grad_w_in, grad_w_out)


def solution(mesh):
    return jax.shard_map(
        shards,
        mesh=mesh,
        in_specs=(
            P(("seq", "head"), None),
            P(("seq", "head"), None),
            P(("seq", "head"), None),
            P(("seq", "head"), None),
            P(("seq", "head"), None),
            P(),
            P(("seq", "head"), None),
            P(("seq", "head"), None),
            P(("seq", "head"), None, None),
            P("seq", None, "head"),
            P("seq", "head", None),
        ),
        out_specs=(
            P(("seq", "head"), None),
            P(("seq", "head"), None),
            P(("seq", "head"), None),
            P(("seq", "head"), None),
            P("seq", None, "head"),
            P("seq", "head", None),
        ),
        check_vma=False,
    )
```
